32 devices in a mesh: fsdp: 32 (over z, y, x, core).
Axes of the slice: x: 2, y: 2, z: 4, core: 2. Of those that a mesh axis runs over, the one named last changes fastest.
Arguments:
- inputs: float32 [64, 145, 768], P('fsdp'), may hold values from -6 to 6
- cotangent: float32 [64, 145, 768], P('fsdp'), may hold values from -6 to 6
- counts: int32 [32], P('fsdp'), may hold values from 1 to 2, as said below
- params: float32 [7090176], P('fsdp'), as said below
- moment_one: float32 [7090176], P('fsdp')
- moment_two: float32 [7090176], P('fsdp')
Outputs:
- outputs: float32 [64, 145, 768], P('fsdp')
- input_grad: float32 [64, 145, 768], P('fsdp')
- param_grad: float32 [7090176], P('fsdp')
- new_params: float32 [7090176], P('fsdp')
- new_moment_one: float32 [7090176], P('fsdp')
- new_moment_two: float32 [7090176], P('fsdp')
The draws below stay inside these ranges and needn't reach their ends.
Inputs may be any that keep to these rules, and one draw needn't show every extreme that they name: `counts`: some device holds 2 images in every draw. `params`: entries past 7087104 are zero.
All inputs are finite; a program needn't handle non-finite values.
Results may differ from the reference program's by a relative error of at most 0.01.
Values may be sent and summed in bfloat16 or wider, within the bound.
No kernel may reach another device: no remote copies, remote signals or barrier semaphores. Data moves between devices by JAX's collectives and lax.ppermute only.
A program may use at most 192 MiB of HBM per device.

```python
import math
import jax
import jax.numpy as jnp
from jax import lax

D = 768
HD = 64
FF = 3072
TOK = 145
SLOTS = 2
IMAGES = 64
PARAMS = 7087104
PTOT = 7090176
N_FSDP = 32


def draw_counts(key, part):
    first, second = jax.random.split(key)
    drawn = jax.random.randint(first, (N_FSDP,), 1, SLOTS + 1)
    chosen = jax.random.randint(second, (), 0, N_FSDP)
    return jnp.where(jnp.arange(N_FSDP) == chosen, SLOTS, drawn).astype(jnp.int32)


def draw_params(key, part):
    position = jnp.arange(PTOT)
    noise = jnp.clip(jax.random.normal(key, (PTOT,), jnp.float32), -4.0, 4.0)
    wide = 1.0 / D ** 0.5
    segments = [(D, 0.1, 1.0), (D, 0.3, 0.0), (3 * D * D, wide, 0.0), (D, 0.3, 0.0), (D, 0.3, 0.0), (D * D, 3.0 * wide, 0.0), (D, 0.3, 0.0), (D, 0.1, 1.0), (D, 0.3, 0.0), (D * FF, wide, 0.0), (FF, 0.3, 0.0), (FF * D, 1.5 / FF ** 0.5, 0.0), (D, 0.3, 0.0)]
    scales = jnp.zeros((PTOT,), jnp.float32)
    bases = jnp.zeros((PTOT,), jnp.float32)
    offset = 0
    for length_now, spread, centre in segments:
        inside = (position >= offset) & (position < offset + length_now)
        scales = jnp.where(inside, spread, scales)
        bases = jnp.where(inside, centre, bases)
        offset += length_now
    return (bases + scales * noise).astype(jnp.float32)


def gradient_sizes():
    position = jnp.arange(PTOT)
    live_rows = IMAGES * TOK * (SLOTS + 1) / (2.0 * SLOTS)
    root_rows = math.sqrt(live_rows)
    segments = [(D, 1.4), (D, 1.4), (3 * D * D, 0.0), (D, 0.35), (D, 1.3), (D * D, 0.3), (D, 1.4), (D, 1.0), (D, 1.0), (D * FF, 0.5), (FF, 0.5), (FF * D, 0.6), (D, 1.0)]
    sizes_now = jnp.ones((PTOT,), jnp.float32)
    offset = 0
    for length_now, factor in segments:
        inside = (position >= offset) & (position < offset + length_now)
        sizes_now = jnp.where(inside, factor, sizes_now)
        offset += length_now
    qkv_start = 2 * D
    column = (position - qkv_start) % (3 * D)
    in_qkv = (position >= qkv_start) & (position < qkv_start + 3 * D * D)
    sizes_now = jnp.where(in_qkv, jnp.where(column < 2 * D, 0.35, 1.3), sizes_now)
    return sizes_now * root_rows


def draw_moment_one(key, part):
    noise = jnp.clip(jax.random.normal(jax.random.fold_in(key, 11), (PTOT,), jnp.float32), -4.0, 4.0)
    return (0.12 * gradient_sizes() * noise).astype(jnp.float32)


def draw_moment_two(key, part):
    spread = jax.random.uniform(jax.random.fold_in(key, 23), (PTOT,), jnp.float32, math.log(0.05), math.log(0.2))
    sizes_now = gradient_sizes()
    return (sizes_now * sizes_now * jnp.exp(spread)).astype(jnp.float32)


def steps_of(rng, dims, cuts, least, largest):
    level, own = 1.0, jax.random.fold_in(rng, 6)
    for dim, blocks in cuts:
        draws = jnp.exp(jax.random.uniform(jax.random.fold_in(own, dim), (blocks,), jnp.float32, least / len(cuts), largest / len(cuts)))
        level = level * jnp.repeat(draws, dims[dim] // blocks).reshape([-1 if axis == dim else 1 for axis in range(len(dims))])
    return level


def gaussian(key, dims, scale, reach, cuts=(), kind=jnp.bfloat16):
    values = scale * jax.random.normal(key, dims, jnp.float32)
    if cuts:
        values = values * steps_of(key, dims, cuts, -0.22, 0.18)
    return jnp.clip(values, -reach, reach).astype(kind)


def setup_inputs(seed: int = 0) -> dict:
    splits = jax.random.split(jax.random.key(seed), 7)
    inputs = gaussian(splits[0], (IMAGES, TOK, D), 1.0, 6.0, ((0, 32),), jnp.float32)
    cotangent = gaussian(splits[1], (IMAGES, TOK, D), 1.0, 6.0, ((0, 32),), jnp.float32)
    counts = draw_counts(jax.random.fold_in(splits[6], 71), 0)
    params = draw_params(jax.random.fold_in(splits[6], 71), 0)
    moment_one = draw_moment_one(jax.random.fold_in(splits[6], 71), 0)
    moment_two = draw_moment_two(jax.random.fold_in(splits[6], 71), 0)
    return dict(inputs=inputs, cotangent=cotangent, counts=counts, params=params, moment_one=moment_one, moment_two=moment_two)


EPS_NORM = 1e-06
BETA_ONE = 0.9
BETA_TWO = 0.95
RATE = 0.01
DECAY = 0.05
EPS_ADAM = 1e-08
ADAM_STEP = 3.0
INV_ROOT_TWO = 0.7071067811865476
INV_ROOT_TWOPI = 0.3989422804014327

def batched(form, left, right):
    return jnp.einsum(form, left.astype(jnp.float32), right.astype(jnp.float32))

def unpack(flat):
    layouts = [(D,), (D,), (D, 3 * D), (D,), (D,), (D, D), (D,), (D,), (D,), (D, FF), (FF,), (FF, D), (D,)]
    pieces = []
    offset = 0
    for layout_now in layouts:
        number = math.prod(layout_now)
        pieces.append(flat[offset:offset + number].reshape(layout_now))
        offset += number
    return pieces

def layer_norm(values, norm_gain, norm_shift):
    centre = values - lax.optimization_barrier(jnp.mean(values, axis=-1, keepdims=True))
    scale_inv = lax.rsqrt(lax.optimization_barrier(jnp.mean(centre * centre, axis=-1, keepdims=True)) + EPS_NORM)
    normed = centre * scale_inv
    return (normed * norm_gain + norm_shift, normed, scale_inv)

def norm_back(grad_out, normed, scale_inv, norm_gain):
    gain_grad = lax.optimization_barrier(jnp.sum(grad_out * normed, axis=(0, 1)))
    shift_grad = lax.optimization_barrier(jnp.sum(grad_out, axis=(0, 1)))
    scaled = grad_out * norm_gain
    back = scale_inv * (scaled - lax.optimization_barrier(jnp.mean(scaled, axis=-1, keepdims=True)) - normed * lax.optimization_barrier(jnp.mean(scaled * normed, axis=-1, keepdims=True)))
    return (back, gain_grad, shift_grad)

def run_block(inputs, cotangent, forward_flat, backward_flat):
    f32 = jnp.float32
    bf16 = jnp.bfloat16
    norm1_gain, norm1_shift, qkv_weight, query_bias, value_bias, out_weight, out_bias, norm2_gain, norm2_shift, hidden_weight, hidden_bias, down_weight, down_bias = unpack(forward_flat)
    image_count, token_count, features = inputs.shape
    row_count = image_count * token_count
    head_count = features // HD
    qk_scale = 1.0 / math.sqrt(HD)
    heads_shape = (image_count, token_count, head_count, HD)
    first_norm, normed_one, inv_one = layer_norm(inputs, norm1_gain.astype(f32), norm1_shift.astype(f32))
    act_one = first_norm.reshape(row_count, features).astype(bf16)
    projected = jnp.dot(act_one, qkv_weight, preferred_element_type=f32)
    query_heads = (projected[:, :features] + query_bias.astype(f32)).astype(bf16).reshape(heads_shape)
    key_heads = projected[:, features:2 * features].astype(bf16).reshape(heads_shape)
    value_heads = (projected[:, 2 * features:] + value_bias.astype(f32)).astype(bf16).reshape(heads_shape)
    scores = batched('sqhd,skhd->shqk', query_heads, key_heads) * qk_scale
    row_max = lax.optimization_barrier(jnp.max(scores, axis=-1, keepdims=True))
    log_total = row_max + jnp.log(lax.optimization_barrier(jnp.sum(jnp.exp(scores - row_max), axis=-1, keepdims=True)))
    attention = jnp.exp(scores - log_total)
    mixed = batched('shqk,skhd->sqhd', attention.astype(bf16), value_heads)
    mixed_rows = mixed.astype(bf16).reshape(row_count, features)
    attn_out = jnp.dot(mixed_rows, out_weight, preferred_element_type=f32) + out_bias.astype(f32)
    middle = inputs + attn_out.reshape(inputs.shape)
    second_norm, normed_two, inv_two = layer_norm(middle, norm2_gain.astype(f32), norm2_shift.astype(f32))
    act_two = second_norm.reshape(row_count, features).astype(bf16)
    pre_act = jnp.dot(act_two, hidden_weight, preferred_element_type=f32) + hidden_bias.astype(f32)
    hidden_rows = jax.nn.gelu(pre_act, approximate=False).astype(bf16)
    outputs = middle + (jnp.dot(hidden_rows, down_weight, preferred_element_type=f32) + down_bias.astype(f32)).reshape(inputs.shape)
    norm1_gain, norm1_shift, qkv_weight, query_bias, value_bias, out_weight, out_bias, norm2_gain, norm2_shift, hidden_weight, hidden_bias, down_weight, down_bias = unpack(backward_flat)
    grad_rows = cotangent.reshape(row_count, features)
    grad_narrow = grad_rows.astype(bf16)
    grad_down = jnp.dot(hidden_rows.T, grad_narrow, preferred_element_type=f32)
    grad_down_bias = lax.optimization_barrier(jnp.sum(grad_rows, axis=0))
    slope = 0.5 * (1.0 + lax.erf(pre_act * INV_ROOT_TWO)) + pre_act * jnp.exp(-0.5 * pre_act * pre_act) * INV_ROOT_TWOPI
    d_pre = jnp.dot(grad_narrow, down_weight.T, preferred_element_type=f32) * slope
    d_pre_narrow = d_pre.astype(bf16)
    grad_hidden = jnp.dot(act_two.T, d_pre_narrow, preferred_element_type=f32)
    grad_hidden_bias = lax.optimization_barrier(jnp.sum(d_pre, axis=0))
    d_act_two = jnp.dot(d_pre_narrow, hidden_weight.T, preferred_element_type=f32).reshape(inputs.shape)
    d_mid_norm, grad_gain_two, grad_shift_two = norm_back(d_act_two, normed_two, inv_two, norm2_gain.astype(f32))
    d_middle = cotangent + d_mid_norm
    d_mid_rows = d_middle.reshape(row_count, features)
    d_mid_narrow = d_mid_rows.astype(bf16)
    grad_out_weight = jnp.dot(mixed_rows.T, d_mid_narrow, preferred_element_type=f32)
    grad_out_bias = lax.optimization_barrier(jnp.sum(d_mid_rows, axis=0))
    d_mixed = jnp.dot(d_mid_narrow, out_weight.T, preferred_element_type=f32).astype(bf16).reshape(heads_shape)
    scores = batched('sqhd,skhd->shqk', query_heads, key_heads) * qk_scale
    attention = jnp.exp(scores - log_total)
    d_attention = batched('sqhd,skhd->shqk', d_mixed, value_heads)
    row_dot = lax.optimization_barrier(jnp.sum(attention * d_attention, axis=-1, keepdims=True))
    d_scores = (attention * (d_attention - row_dot) * qk_scale).astype(bf16)
    d_query = batched('shqk,skhd->sqhd', d_scores, key_heads).reshape(row_count, features)
    d_keys = batched('shqk,sqhd->skhd', d_scores, query_heads).reshape(row_count, features)
    d_values = batched('shqk,sqhd->skhd', attention.astype(bf16), d_mixed).reshape(row_count, features)
    d_proj_narrow = jnp.concatenate([d_query, d_keys, d_values], axis=1).astype(bf16)
    grad_qkv = jnp.dot(act_one.T, d_proj_narrow, preferred_element_type=f32)
    grad_query_bias = lax.optimization_barrier(jnp.sum(d_query, axis=0))
    grad_value_bias = lax.optimization_barrier(jnp.sum(d_values, axis=0))
    d_act_one = jnp.dot(d_proj_narrow, qkv_weight.T, preferred_element_type=f32).reshape(inputs.shape)
    d_in_norm, grad_gain_one, grad_shift_one = norm_back(d_act_one, normed_one, inv_one, norm1_gain.astype(f32))
    input_grad = d_middle + d_in_norm
    grads = jnp.concatenate([grad_gain_one, grad_shift_one, grad_qkv.reshape(-1), grad_query_bias, grad_value_bias, grad_out_weight.reshape(-1), grad_out_bias, grad_gain_two, grad_shift_two, grad_hidden.reshape(-1), grad_hidden_bias, grad_down.reshape(-1), grad_down_bias])
    return (outputs, input_grad, grads)

def adam_update(params, grads, moment_one, moment_two):
    new_one = BETA_ONE * moment_one + (1.0 - BETA_ONE) * grads
    new_two = BETA_TWO * moment_two + (1.0 - BETA_TWO) * grads * grads
    fix_one = 1.0 - BETA_ONE ** ADAM_STEP
    fix_two = 1.0 - BETA_TWO ** ADAM_STEP
    update = new_one / fix_one / (jnp.sqrt(new_two / fix_two) + EPS_ADAM)
    return (params - RATE * (update + DECAY * params), new_one, new_two)

def reference(inputs, cotangent, counts, params, moment_one, moment_two):
    live_slots = (jnp.arange(SLOTS)[None, :] < counts[:, None]).reshape(-1).astype(jnp.float32)
    masked = cotangent * live_slots[:, None, None]
    narrow = params.astype(jnp.bfloat16)
    group_size = SLOTS * 8
    blocks = IMAGES // group_size

    def step_block(grad_total, block_pair):
        block_out, block_grad, grads = run_block(block_pair[0], block_pair[1], narrow, narrow)
        return (grad_total + grads, (block_out, block_grad))
    grad_total, (outs_all, grads_all) = lax.scan(step_block, jnp.zeros((PARAMS,), jnp.float32), (inputs.reshape(blocks, group_size, TOK, D), masked.reshape(blocks, group_size, TOK, D)))
    param_grad = jnp.concatenate([grad_total, jnp.zeros((PTOT - PARAMS,), jnp.float32)])
    new_params, new_one, new_two = adam_update(params, param_grad, moment_one, moment_two)
    return (outs_all.reshape(IMAGES, TOK, D), grads_all.reshape(IMAGES, TOK, D), param_grad, new_params, new_one, new_two)
```

```python
import functools
import math

import jax
import jax.numpy as jnp
from jax import lax
from jax.experimental import pallas as pl
from jax.experimental.pallas import tpu as pltpu
from jax.sharding import PartitionSpec as P

D = 768
HD = 64
FF = 3072
PARAMS = 7087104
LANES = 128
TPAD = 384

EPS_NORM = 1e-06
BETA_ONE = 0.9
BETA_TWO = 0.95
RATE = 0.01
DECAY = 0.05
EPS_ADAM = 1e-08
ADAM_STEP = 3.0
INV_ROOT_TWO = 0.7071067811865476
INV_ROOT_TWOPI = 0.3989422804014327
F32 = jnp.float32
BF16 = jnp.bfloat16

SEGMENTS = (
    ("g1", 1, 6),
    ("c1", 1, 6),
    ("wqkv", D, 18),
    ("bq", 1, 6),
    ("bv", 1, 6),
    ("wo", D, 6),
    ("bo", 1, 6),
    ("g2", 1, 6),
    ("c2", 1, 6),
    ("w1", D, 24),
    ("b1", 1, 24),
    ("w2", FF, 6),
    ("b2", 1, 6),
)
GROUPS = (("g1", "c1", "wqkv", "bq", "bv"), ("wo", "bo", "g2", "c2"), ("w1", "b1"), ("w2", "b2"))
OFFSETS = {}
SHAPES = {}
_at = 0
for _name, _k, _j in SEGMENTS:
    OFFSETS[_name] = _at
    SHAPES[_name] = (_k, _j)
    _at += _k * _j
USED_ROWS = _at


def round_up(value, step):
    return -(-value // step) * step


class Plan:
    def __init__(self, devices, shard):
        self.devices = devices
        self.bits = devices.bit_length() - 1
        self.rows = shard // LANES
        self.padded = round_up(self.rows, 16)
        half = round_up(self.padded // 2, 16)
        self.halves = ((0, half), (half, self.padded))
        self.quarters = 4
        self.low = devices // self.quarters
        self.low_bits = self.bits - 2

    def low_order(self, half):
        order = [1, 2] if half == 0 else [2, 1]
        return list(range(self.low_bits - 1, 2, -1)) + order + [0]


def exchange(array, mask, devices):
    return lax.ppermute(array, "fsdp", [(i, i ^ mask) for i in range(devices)])


def gather_quarters(narrow, plan, me):
    quarter = me // plan.low
    result = [[None, None] for _ in range(plan.quarters)]
    for half, (lo, hi) in enumerate(plan.halves):
        part = narrow[None, None, lo:hi]
        for axis, bit in ((0, plan.bits - 1), (1, plan.bits - 2)):
            part = jnp.concatenate([part, exchange(part, 1 << bit, plan.devices)], axis=axis)
        part = part.reshape((plan.quarters,) + part.shape[2:])
        for q in range(plan.quarters):
            block = lax.dynamic_index_in_dim(part, quarter ^ q, 0, keepdims=False)
            block = block.reshape((1,) * plan.low_bits + block.shape)
            for bit in plan.low_order(half):
                axis = plan.low_bits - 1 - bit
                block = jnp.concatenate([block, exchange(block, 1 << bit, plan.devices)], axis=axis)
            result[q][half] = block.reshape((plan.low,) + block.shape[-2:])
    return result


def unpack_group(names, gathered, plan, position):
    start = OFFSETS[names[0]]
    stop = OFFSETS[names[-1]] + math.prod(SHAPES[names[-1]])
    first, last = start // plan.rows, (stop - 1) // plan.rows
    count = last - first + 1
    quarters = list(range(first // plan.low, last // plan.low + 1))
    flat_rows = round_up(stop - start, 8) + 8

    def kernel(*refs):
        position_ref = refs[0]
        sources = refs[1 : 1 + 2 * len(quarters)]
        outs = refs[1 + 2 * len(quarters) : -3]
        stage, flat, sems = refs[-3:]
        mine = position_ref[0]
        copies = []
        for i in range(count):
            device = first + i
            q = device // plan.low - quarters[0]
            spot = (device % plan.low) ^ mine
            for half, (lo, hi) in enumerate(plan.halves):
                copy = pltpu.make_async_copy(
                    sources[2 * q + half].at[spot], stage.at[i, lo:hi], sems.at[i, half]
                )
                copy.start()
                copies.append(copy)
        for i in range(count):
            copies[2 * i].wait()
            copies[2 * i + 1].wait()
            base = (first + i) * plan.rows
            row = max(start, base)
            end = min(stop, base + plan.rows)
            while row < end:
                inside = row - base
                lower = inside // 16 * 16
                upper = min(lower + 256, end - base)
                block = stage[i, lower : round_up(upper, 16), :].astype(F32)
                flat[row - start : base + upper - start, :] = block[inside - lower : upper - lower]
                row = base + upper
        for name, out in zip(names, outs):
            rows, blocks = SHAPES[name]
            offset = OFFSETS[name] - start
            if rows == 1:
                for j in range(blocks):
                    out[:, j * LANES : (j + 1) * LANES] = flat[offset + j : offset + j + 1, :]
            else:

                @pl.loop(0, blocks)
                def _(j, out=out, rows=rows, blocks=blocks, offset=offset):
                    column = flat[pl.ds(offset + j, rows, stride=blocks), :]
                    out[:, pl.ds(pl.multiple_of(j * LANES, LANES), LANES)] = column.astype(BF16)

    shapes = []
    for name in names:
        rows, blocks = SHAPES[name]
        kind = F32 if rows == 1 else BF16
        shapes.append(jax.ShapeDtypeStruct((rows, blocks * LANES), kind))
    operands = [gathered[q][half] for q in quarters for half in range(2)]
    results = pl.pallas_call(
        kernel,
        out_shape=shapes,
        in_specs=[pl.BlockSpec(memory_space=pltpu.SMEM)]
        + [pl.BlockSpec(memory_space=pl.ANY)] * len(operands),
        out_specs=[pl.BlockSpec(memory_space=pltpu.VMEM)] * len(shapes),
        scratch_shapes=[
            pltpu.VMEM((count, plan.padded, LANES), BF16),
            pltpu.VMEM((flat_rows, LANES), F32),
            pltpu.SemaphoreType.DMA((count, 2)),
        ],
        cost_estimate=pl.CostEstimate(
            flops=0, bytes_accessed=4 * (stop - start) * LANES, transcendentals=0
        ),
        name="unpack_" + names[0],
    )(position, *operands)
    return dict(zip(names, results))


def pack_quarter(quarter, factors, vectors, plan):
    start = quarter * plan.low * plan.rows
    stop = start + plan.low * plan.rows
    pieces = []
    base, top = start, stop
    for name, rows, blocks in SEGMENTS:
        offset = OFFSETS[name]
        lo, hi = max(start, offset), min(stop, offset + rows * blocks)
        if lo >= hi:
            continue
        if rows == 1:
            pieces.append((name, offset, lo - offset, hi - offset))
        else:
            k0 = (lo - offset) // blocks // LANES * LANES
            k1 = round_up(-(-(hi - offset) // blocks), LANES)
            pieces.append((name, offset, k0, k1))
            base = min(base, offset + k0 * blocks)
            top = max(top, offset + k1 * blocks)
    flat_rows = round_up(top - base, 8) + 32
    operands = []
    for name, *_ in pieces:
        operands.extend(factors[name] if name in factors else (vectors[name],))

    def kernel(*refs):
        ins = list(refs[: len(operands)])
        outs = refs[len(operands) : len(operands) + 2]
        flat, turned = refs[len(operands) + 2 :]
        for name, offset, lo, hi in pieces:
            rows, blocks = SHAPES[name]
            if rows == 1:
                row_ref = ins.pop(0)
                for j in range(lo, hi):
                    at = offset + j - base
                    flat[at : at + 1, :] = row_ref[:, j * LANES : (j + 1) * LANES]
                continue
            left, right = ins.pop(0), ins.pop(0)
            size = hi - lo
            step = 256 if size % 256 == 0 else 128
            for k in range(lo, hi, 128):
                turned[k - lo : k - lo + 128, :] = left[:, k : k + 128].T

            @pl.loop(0, blocks // 2)
            def _(pair, right=right, lo=lo, size=size, step=step, offset=offset, blocks=blocks):
                columns = right[:, pl.ds(pl.multiple_of(pair * 256, 256), 256)]

                @pl.loop(0, size // step)
                def _(part):
                    k = pl.multiple_of(part * step, step)
                    product = jnp.dot(
                        turned[pl.ds(k, step), :], columns, preferred_element_type=F32
                    )
                    at = offset - base + (lo + k) * blocks + 2 * pair
                    flat[pl.ds(at, step, stride=blocks), :] = product[:, :LANES]
                    flat[pl.ds(at + 1, step, stride=blocks), :] = product[:, LANES:]

        if stop > USED_ROWS:
            flat[max(start, USED_ROWS) - base : stop - base, :] = jnp.zeros(
                (stop - max(start, USED_ROWS), LANES), F32
            )
        for i in range(plan.low):
            for (lo, hi), out in zip(plan.halves, outs):
                for row in range(lo, hi, 256):
                    end = min(row + 256, hi)
                    at = start - base + i * plan.rows
                    out[i, row - lo : end - lo, :] = flat[at + row : at + end, :].astype(BF16)

    widest = max([hi - lo for name, _, lo, hi in pieces if SHAPES[name][0] > 1] + [128])
    return pl.pallas_call(
        kernel,
        out_shape=[
            jax.ShapeDtypeStruct((plan.low, hi - lo, LANES), BF16) for lo, hi in plan.halves
        ],
        in_specs=[pl.BlockSpec(memory_space=pltpu.VMEM)] * len(operands),
        out_specs=[pl.BlockSpec(memory_space=pltpu.VMEM)] * 2,
        scratch_shapes=[pltpu.VMEM((flat_rows, LANES), F32), pltpu.VMEM((widest, TPAD), BF16)],
        cost_estimate=pl.CostEstimate(
            flops=2 * (top - base) * LANES * TPAD,
            bytes_accessed=4 * (top - base) * LANES,
            transcendentals=0,
        ),
        name=f"pack_{quarter}",
    )(*operands)


def halve(array, axis, bit, plan, me, last=False):
    mine = (me >> bit) & 1
    keep = lax.dynamic_index_in_dim(array, mine, axis, keepdims=False)
    send = lax.dynamic_index_in_dim(array, 1 - mine, axis, keepdims=False)
    total = keep.astype(F32) + exchange(send, 1 << bit, plan.devices).astype(F32)
    return total if last else total.astype(BF16)


def scatter_quarters(packed, plan, me):
    parts = []
    for half in range(2):
        blocks = []
        for q in range(plan.quarters):
            block = packed[q][half]
            block = block.reshape((2,) * plan.low_bits + block.shape[1:])
            left = list(range(plan.low_bits - 1, -1, -1))
            for bit in reversed(plan.low_order(half)):
                block = halve(block, left.index(bit), bit, plan, me)
                left.remove(bit)
            blocks.append(block)
        stacked = jnp.stack(blocks).reshape((2, 2) + blocks[0].shape)
        stacked = halve(stacked, 1, plan.bits - 2, plan, me)
        parts.append(halve(stacked, 0, plan.bits - 1, plan, me, last=True))
    return jnp.concatenate(parts, axis=0)[: plan.rows]


def batched(form, left, right):
    return jnp.einsum(form, left, right, preferred_element_type=F32)


def layer_norm(values, norm_gain, norm_shift):
    centre = values - jnp.mean(values, axis=-1, keepdims=True)
    scale_inv = lax.rsqrt(jnp.mean(centre * centre, axis=-1, keepdims=True) + EPS_NORM)
    normed = centre * scale_inv
    return (normed * norm_gain + norm_shift, normed, scale_inv)


def norm_back(grad_out, normed, scale_inv, norm_gain):
    gain_grad = jnp.sum(grad_out * normed, axis=(0, 1))
    shift_grad = jnp.sum(grad_out, axis=(0, 1))
    scaled = grad_out * norm_gain
    back = scale_inv * (
        scaled
        - jnp.mean(scaled, axis=-1, keepdims=True)
        - normed * jnp.mean(scaled * normed, axis=-1, keepdims=True)
    )
    return (back, gain_grad, shift_grad)


def run_block(inputs, cotangent, w):
    image_count, token_count, features = inputs.shape
    row_count = image_count * token_count
    head_count = features // HD
    qk_scale = 1.0 / math.sqrt(HD)
    heads_shape = (image_count, token_count, head_count, HD)
    first_norm, normed_one, inv_one = layer_norm(inputs, w["g1"], w["c1"])
    act_one = first_norm.reshape(row_count, features).astype(BF16)
    projected = jnp.dot(act_one, w["wqkv"], preferred_element_type=F32)
    query_heads = (projected[:, :features] + w["bq"]).astype(BF16).reshape(heads_shape)
    key_heads = projected[:, features : 2 * features].astype(BF16).reshape(heads_shape)
    value_heads = (projected[:, 2 * features :] + w["bv"]).astype(BF16).reshape(heads_shape)
    scores = batched("sqhd,skhd->shqk", query_heads, key_heads) * qk_scale
    row_max = jnp.max(scores, axis=-1, keepdims=True)
    log_total = row_max + jnp.log(jnp.sum(jnp.exp(scores - row_max), axis=-1, keepdims=True))
    attention = jnp.exp(scores - log_total)
    mixed = batched("shqk,skhd->sqhd", attention.astype(BF16), value_heads)
    mixed_rows = mixed.astype(BF16).reshape(row_count, features)
    attn_out = jnp.dot(mixed_rows, w["wo"], preferred_element_type=F32) + w["bo"]
    middle = inputs + attn_out.reshape(inputs.shape)
    second_norm, normed_two, inv_two = layer_norm(middle, w["g2"], w["c2"])
    act_two = second_norm.reshape(row_count, features).astype(BF16)
    pre_act = jnp.dot(act_two, w["w1"], preferred_element_type=F32) + w["b1"]
    hidden_rows = jax.nn.gelu(pre_act, approximate=False).astype(BF16)
    outputs = middle + (
        jnp.dot(hidden_rows, w["w2"], preferred_element_type=F32) + w["b2"]
    ).reshape(inputs.shape)
    grad_rows = cotangent.reshape(row_count, features)
    grad_narrow = grad_rows.astype(BF16)
    slope = (
        0.5 * (1.0 + lax.erf(pre_act * INV_ROOT_TWO))
        + pre_act * jnp.exp(-0.5 * pre_act * pre_act) * INV_ROOT_TWOPI
    )
    d_pre = jnp.dot(grad_narrow, w["w2"].T, preferred_element_type=F32) * slope
    d_pre_narrow = d_pre.astype(BF16)
    d_act_two = jnp.dot(d_pre_narrow, w["w1"].T, preferred_element_type=F32).reshape(inputs.shape)
    d_mid_norm, grad_gain_two, grad_shift_two = norm_back(d_act_two, normed_two, inv_two, w["g2"])
    d_middle = cotangent + d_mid_norm
    d_mid_rows = d_middle.reshape(row_count, features)
    d_mid_narrow = d_mid_rows.astype(BF16)
    d_mixed = (
        jnp.dot(d_mid_narrow, w["wo"].T, preferred_element_type=F32)
        .astype(BF16)
        .reshape(heads_shape)
    )
    d_attention = batched("sqhd,skhd->shqk", d_mixed, value_heads)
    row_dot = jnp.sum(attention * d_attention, axis=-1, keepdims=True)
    d_scores = (attention * (d_attention - row_dot) * qk_scale).astype(BF16)
    d_query = batched("shqk,skhd->sqhd", d_scores, key_heads).reshape(row_count, features)
    d_keys = batched("shqk,sqhd->skhd", d_scores, query_heads).reshape(row_count, features)
    d_values = batched("shqk,sqhd->skhd", attention.astype(BF16), d_mixed).reshape(
        row_count, features
    )
    d_proj_narrow = jnp.concatenate([d_query, d_keys, d_values], axis=1).astype(BF16)
    d_act_one = jnp.dot(d_proj_narrow, w["wqkv"].T, preferred_element_type=F32).reshape(
        inputs.shape
    )
    d_in_norm, grad_gain_one, grad_shift_one = norm_back(d_act_one, normed_one, inv_one, w["g1"])
    input_grad = d_middle + d_in_norm
    pad = lambda rows: jnp.pad(rows, ((0, TPAD - row_count), (0, 0)))
    factors = {
        "wqkv": (pad(act_one), pad(d_proj_narrow)),
        "wo": (pad(mixed_rows), pad(d_mid_narrow)),
        "w1": (pad(act_two), pad(d_pre_narrow)),
        "w2": (pad(hidden_rows), pad(grad_narrow)),
    }
    vectors = {
        "g1": grad_gain_one,
        "c1": grad_shift_one,
        "bq": jnp.sum(d_query, axis=0),
        "bv": jnp.sum(d_values, axis=0),
        "bo": jnp.sum(d_mid_rows, axis=0),
        "g2": grad_gain_two,
        "c2": grad_shift_two,
        "b1": jnp.sum(d_pre, axis=0),
        "b2": jnp.sum(grad_rows, axis=0),
    }
    vectors = {name: value.reshape(1, -1) for name, value in vectors.items()}
    return (outputs, input_grad, factors, vectors)


def adam_update(params, grads, moment_one, moment_two):
    new_one = BETA_ONE * moment_one + (1.0 - BETA_ONE) * grads
    new_two = BETA_TWO * moment_two + (1.0 - BETA_TWO) * grads * grads
    fix_one = 1.0 - BETA_ONE**ADAM_STEP
    fix_two = 1.0 - BETA_TWO**ADAM_STEP
    update = new_one / fix_one / (jnp.sqrt(new_two / fix_two) + EPS_ADAM)
    return (params - RATE * (update + DECAY * params), new_one, new_two)


def local(plan, inputs, cotangent, counts, params, moment_one, moment_two):
    me = lax.axis_index("fsdp")
    live_slots = (jnp.arange(inputs.shape[0]) < counts[0]).astype(F32)
    masked = cotangent * live_slots[:, None, None]
    rows = params.reshape(plan.rows, LANES)
    narrow = jnp.pad(rows.astype(BF16), ((0, plan.padded - plan.rows), (0, 0)))
    gathered = gather_quarters(narrow, plan, me)
    position = (me % plan.low).astype(jnp.int32).reshape(1)
    weights = {}
    for names in GROUPS:
        weights.update(unpack_group(names, gathered, plan, position))
    outputs, input_grad, factors, vectors = run_block(inputs, masked, weights)
    packed = [pack_quarter(q, factors, vectors, plan) for q in range(plan.quarters)]
    shard_grad = scatter_quarters(packed, plan, me)
    new_params, new_one, new_two = adam_update(
        rows,
        shard_grad,
        moment_one.reshape(plan.rows, LANES),
        moment_two.reshape(plan.rows, LANES),
    )
    flat = lambda array: array.reshape(-1)
    return (outputs, input_grad, flat(shard_grad), flat(new_params), flat(new_one), flat(new_two))


def solution(mesh):
    devices = mesh.shape["fsdp"]

    def step(inputs, cotangent, counts, params, moment_one, moment_two):
        plan = Plan(devices, params.shape[0] // devices)
        placed = (P("fsdp", None, None),) * 2 + (P("fsdp"),) * 4
        return jax.shard_map(
            functools.partial(local, plan),
            mesh=mesh,
            in_specs=placed,
            out_specs=placed,
            check_vma=False,
        )(inputs, cotangent, counts, params, moment_one, moment_two)

    return step
```

```python
import functools
import math

import jax
import jax.numpy as jnp
from jax import lax
from jax.experimental import pallas as pl
from jax.experimental.pallas import tpu as pltpu
from jax.sharding import PartitionSpec as P


D = 768
HD = 64
FF = 3072
LANES = 128

EPS_NORM = 1e-06
BETA_ONE = 0.9
BETA_TWO = 0.95
RATE = 0.01
DECAY = 0.05
EPS_ADAM = 1e-08
ADAM_STEP = 3.0
INV_ROOT_TWO = 0.7071067811865476
INV_ROOT_TWOPI = 0.3989422804014327
F32 = jnp.float32
BF16 = jnp.bfloat16

SEGMENTS = (
    ("g1", 1, 6),
    ("c1", 1, 6),
    ("wqkv", D, 18),
    ("bq", 1, 6),
    ("bv", 1, 6),
    ("wo", D, 6),
    ("bo", 1, 6),
    ("g2", 1, 6),
    ("c2", 1, 6),
    ("w1", D, 24),
    ("b1", 1, 24),
    ("w2", FF, 6),
    ("b2", 1, 6),
)
GROUPS = (("g1", "c1", "wqkv", "bq", "bv"), ("wo", "bo", "g2", "c2"), ("w1", "b1"), ("w2", "b2"))
OFFSETS = {}
SHAPES = {}
_at = 0
for _name, _k, _j in SEGMENTS:
    OFFSETS[_name] = _at
    SHAPES[_name] = (_k, _j)
    _at += _k * _j
USED_ROWS = _at


def round_up(value, step):
    return -(-value // step) * step


class Plan:
    def __init__(self, devices, shard):
        self.devices = devices
        self.bits = devices.bit_length() - 1
        self.rows = shard // LANES
        self.padded = round_up(self.rows, 16)
        half = round_up(self.padded // 2, 16)
        self.halves = ((0, half), (half, self.padded))
        self.quarters = 4
        self.low = devices // self.quarters
        self.low_bits = self.bits - 2

    def low_order(self, half):
        order = [1, 2] if half == 0 else [2, 1]
        return list(range(self.low_bits - 1, 2, -1)) + order + [0]


def exchange(array, mask, devices):
    return lax.ppermute(array, "fsdp", [(i, i ^ mask) for i in range(devices)])


def tie(first, second):
    return lax.optimization_barrier((first, second))


def gather_quarters(narrow, plan, me):
    quarter = me // plan.low
    result = [[None, None] for _ in range(plan.quarters)]
    high = []
    first = None
    for half, (lo, hi) in enumerate(plan.halves):
        part = narrow[None, None, lo:hi]
        if first is not None:
            first, part = tie(first, part)
        part_in = part
        other = exchange(part_in, 1 << (plan.bits - 1), plan.devices)
        if half == 0:
            first = other
        high.append([part_in, other])
    high[0][1] = first
    for half in range(2):
        part = jnp.concatenate(high[half], axis=0)
        other = exchange(part, 1 << (plan.bits - 2), plan.devices)
        part = jnp.concatenate([part, other], axis=1)
        high[half] = part.reshape((plan.quarters,) + part.shape[2:])
    for q in range(plan.quarters):
        for half in range(2):
            block = lax.dynamic_index_in_dim(high[half], quarter ^ q, 0, keepdims=False)
            block = block.reshape((1,) * (plan.low_bits - 1) + block.shape)
            for bit in plan.low_order(half):
                other = exchange(block, 1 << bit, plan.devices)
                if bit:
                    axis = plan.low_bits - 1 - bit
                    block = jnp.concatenate([block, other], axis=axis)
            shape = (plan.low // 2,) + block.shape[-2:]
            result[q][half] = (block.reshape(shape), other.reshape(shape))
    return result


def unpack_group(names, gathered, plan, position):
    start = OFFSETS[names[0]]
    stop = OFFSETS[names[-1]] + math.prod(SHAPES[names[-1]])
    first, last = start // plan.rows, (stop - 1) // plan.rows
    count = last - first + 1
    quarters = list(range(first // plan.low, last // plan.low + 1))
    flat_rows = round_up(stop - start, 8) + 8

    def kernel(*refs):
        position_ref = refs[0]
        sources = refs[1 : 1 + 4 * len(quarters)]
        outs = refs[1 + 4 * len(quarters) : -3]
        stage, flat, sems = refs[-3:]
        mine = position_ref[0]
        copies = []
        for i in range(count):
            device = first + i
            q = device // plan.low - quarters[0]
            spot = (device % plan.low) ^ mine
            for half, (lo, hi) in enumerate(plan.halves):
                for core in range(2):
                    copy = pltpu.make_async_copy(
                        sources[4 * q + 2 * half + core].at[spot // 2],
                        stage.at[i, lo:hi],
                        sems.at[i, half],
                    )
                    pl.when(spot % 2 == core)(copy.start)
                copies.append(copy)
        for i in range(count):
            copies[2 * i].wait()
            copies[2 * i + 1].wait()
            base = (first + i) * plan.rows
            row = max(start, base)
            end = min(stop, base + plan.rows)
            while row < end:
                inside = row - base
                lower = inside // 16 * 16
                upper = min(lower + 256, end - base)
                block = stage[i, lower : round_up(upper, 16), :].astype(F32)
                flat[row - start : base + upper - start, :] = block[inside - lower : upper - lower]
                row = base + upper
        for name, out in zip(names, outs):
            rows, blocks = SHAPES[name]
            offset = OFFSETS[name] - start
            if rows == 1:
                for j in range(blocks):
                    out[:, j * LANES : (j + 1) * LANES] = flat[offset + j : offset + j + 1, :]
            else:

                @pl.loop(0, blocks)
                def _(j, out=out, rows=rows, blocks=blocks, offset=offset):
                    column = flat[pl.ds(offset + j, rows, stride=blocks), :]
                    out[:, pl.ds(pl.multiple_of(j * LANES, LANES), LANES)] = column.astype(BF16)

    shapes = []
    for name in names:
        rows, blocks = SHAPES[name]
        kind = F32 if rows == 1 else BF16
        shapes.append(jax.ShapeDtypeStruct((rows, blocks * LANES), kind))
    operands = [
        gathered[q][half][core] for q in quarters for half in range(2) for core in range(2)
    ]
    results = pl.pallas_call(
        kernel,
        out_shape=shapes,
        in_specs=[pl.BlockSpec(memory_space=pltpu.SMEM)]
        + [pl.BlockSpec(memory_space=pl.ANY)] * len(operands),
        out_specs=[pl.BlockSpec(memory_space=pltpu.VMEM)] * len(shapes),
        scratch_shapes=[
            pltpu.VMEM((count, plan.padded, LANES), BF16),
            pltpu.VMEM((flat_rows, LANES), F32),
            pltpu.SemaphoreType.DMA((count, 2)),
        ],
        cost_estimate=pl.CostEstimate(
            flops=0, bytes_accessed=4 * (stop - start) * LANES, transcendentals=0
        ),
    )(position, *operands)
    return dict(zip(names, results))


def pack_quarter(quarter, factors, vectors, plan):
    start = quarter * plan.low * plan.rows
    stop = start + plan.low * plan.rows
    pieces = []
    base, top = start, stop
    for name, rows, blocks in SEGMENTS:
        offset = OFFSETS[name]
        lo, hi = max(start, offset), min(stop, offset + rows * blocks)
        if lo >= hi:
            continue
        if rows == 1:
            pieces.append((name, offset, lo - offset, hi - offset))
        else:
            k0 = (lo - offset) // blocks // LANES * LANES
            k1 = round_up(-(-(hi - offset) // blocks), LANES)
            pieces.append((name, offset, k0, k1))
            base = min(base, offset + k0 * blocks)
            top = max(top, offset + k1 * blocks)
    flat_rows = round_up(top - base, 8) + 32
    operands = []
    for name, *_ in pieces:
        operands.extend(factors[name] if name in factors else (vectors[name],))

    def kernel(*refs):
        ins = list(refs[: len(operands)])
        outs = refs[len(operands) : len(operands) + 2]
        flat, turned = refs[len(operands) + 2 :]
        for name, offset, lo, hi in pieces:
            rows, blocks = SHAPES[name]
            if rows == 1:
                row_ref = ins.pop(0)
                for j in range(lo, hi):
                    at = offset + j - base
                    flat[at : at + 1, :] = row_ref[:, j * LANES : (j + 1) * LANES]
                continue
            left, right = ins.pop(0), ins.pop(0)
            size = hi - lo
            step = 256 if size % 256 == 0 else 128
            for k in range(lo, hi, 128):
                turned[k - lo : k - lo + 128, :] = left[:, k : k + 128].T

            @pl.loop(0, blocks // 2)
            def _(pair, right=right, lo=lo, size=size, step=step, offset=offset, blocks=blocks):
                columns = right[:, pl.ds(pl.multiple_of(pair * 256, 256), 256)]

                @pl.loop(0, size // step)
                def _(part):
                    k = pl.multiple_of(part * step, step)
                    product = jnp.dot(
                        turned[pl.ds(k, step), :], columns, preferred_element_type=F32
                    )
                    at = offset - base + (lo + k) * blocks + 2 * pair
                    flat[pl.ds(at, step, stride=blocks), :] = product[:, :LANES]
                    flat[pl.ds(at + 1, step, stride=blocks), :] = product[:, LANES:]

        if stop > USED_ROWS:
            flat[max(start, USED_ROWS) - base : stop - base, :] = jnp.zeros(
                (stop - max(start, USED_ROWS), LANES), F32
            )
        for i in range(plan.low):
            for (lo, hi), out in zip(plan.halves, outs):
                for row in range(lo, hi, 256):
                    end = min(row + 256, hi)
                    at = start - base + i * plan.rows
                    out[i, row - lo : end - lo, :] = flat[at + row : at + end, :].astype(BF16)

    length = factors["w2"][0].shape[0]
    widest = max([hi - lo for name, _, lo, hi in pieces if SHAPES[name][0] > 1] + [128])
    return pl.pallas_call(
        kernel,
        out_shape=[
            jax.ShapeDtypeStruct((plan.low, hi - lo, LANES), BF16) for lo, hi in plan.halves
        ],
        in_specs=[pl.BlockSpec(memory_space=pltpu.VMEM)] * len(operands),
        out_specs=[pl.BlockSpec(memory_space=pltpu.VMEM)] * 2,
        scratch_shapes=[pltpu.VMEM((flat_rows, LANES), F32), pltpu.VMEM((widest, length), BF16)],
        cost_estimate=pl.CostEstimate(
            flops=2 * (top - base) * LANES * length,
            bytes_accessed=4 * (top - base) * LANES,
            transcendentals=0,
        ),
    )(*operands)


def halve(array, axis, bit, plan, me, last=False):
    mine = (me >> bit) & 1
    keep = lax.dynamic_index_in_dim(array, mine, axis, keepdims=False)
    send = lax.dynamic_index_in_dim(array, 1 - mine, axis, keepdims=False)
    got = exchange(send, 1 << bit, plan.devices)
    total = keep.astype(F32) + got.astype(F32)
    return total if last else total.astype(BF16)


def scatter_quarter(packed, plan, me):
    blocks = []
    for half in range(2):
        block = packed[half]
        block = block.reshape((2,) * plan.low_bits + block.shape[1:])
        left = list(range(plan.low_bits - 1, -1, -1))
        for bit in reversed(plan.low_order(half)):
            block = halve(block, left.index(bit), bit, plan, me)
            left.remove(bit)
        blocks.append(block)
    return blocks


def scatter_across(blocks, plan, me):
    parts = []
    for half in range(2):
        stacked = jnp.stack([blocks[q][half] for q in range(plan.quarters)])
        stacked = stacked.reshape((2, 2) + stacked.shape[1:])
        stacked = halve(stacked, 1, plan.bits - 2, plan, me)
        parts.append(halve(stacked, 0, plan.bits - 1, plan, me, last=True))
    return jnp.concatenate(parts, axis=0)[: plan.rows]


NT = (((1,), (1,)), ((), ()))
TN = (((0,), (0,)), ((), ()))
CHUNK = 32


def dot(left, right, numbers=(((1,), (0,)), ((), ()))):
    return lax.dot_general(left, right, numbers, preferred_element_type=F32)


def call(kernel, shapes, operands, scratch=(), scalars=0, flops=0):
    space = [pltpu.SMEM] * scalars + [pltpu.VMEM] * (len(operands) - scalars)
    moved = sum(math.prod(a.shape) * a.dtype.itemsize for a in list(operands) + list(shapes))
    return pl.pallas_call(
        kernel,
        out_shape=shapes,
        in_specs=[pl.BlockSpec(memory_space=s) for s in space],
        out_specs=[pl.BlockSpec(memory_space=pltpu.VMEM)] * len(shapes),
        scratch_shapes=list(scratch),
        cost_estimate=pl.CostEstimate(flops=flops, bytes_accessed=moved, transcendentals=0),
    )(*operands)


def array(shape, kind=F32):
    return jax.ShapeDtypeStruct(shape, kind)


def row_norm(values):
    centre = values - jnp.mean(values, axis=-1, keepdims=True)
    scale_inv = lax.rsqrt(jnp.mean(centre * centre, axis=-1, keepdims=True) + EPS_NORM)
    return centre * scale_inv, scale_inv


def row_norm_back(grad, values, gain):
    normed, scale_inv = row_norm(values)
    scaled = grad * gain
    back = scale_inv * (
        scaled
        - jnp.mean(scaled, axis=-1, keepdims=True)
        - normed * jnp.mean(scaled * normed, axis=-1, keepdims=True)
    )
    return back, jnp.sum(grad * normed, axis=0, keepdims=True)


def rows_of(index, size=CHUNK):
    return pl.ds(pl.multiple_of(index * size, size), size)


def fill_padded(target, source, stride):
    slots, tokens, _ = source.shape
    target[...] = jnp.zeros_like(target)
    for s in range(slots):
        target[s * stride : s * stride + tokens, :] = source[s]


def fill_masked(target, source, count, stride):
    slots, tokens, _ = source.shape
    target[...] = jnp.zeros_like(target)
    for s in range(slots):
        live = jnp.where(s < count, 1.0, 0.0).astype(F32)
        target[s * stride : s * stride + tokens, :] = source[s] * live


def run_block(counts, inputs, cotangent, w, pack):
    slots, tokens, _ = inputs.shape
    stride = round_up(tokens, 16)
    total = slots * stride
    heads = D // HD
    pairs = heads // 2
    qk_scale = 1.0 / math.sqrt(HD)

    def head_rows(i):
        return pl.ds(pl.multiple_of(i // pairs * stride, 16), stride)

    def head_columns(i, part):
        return pl.ds(pl.multiple_of(part * D + i % pairs * LANES, LANES), LANES)

    def lane_mask(part):
        lane = lax.broadcasted_iota(jnp.int32, (stride, LANES), 1)
        return (lane < HD) if part == 0 else (lane >= HD)

    def attend(count, x, cot, g1, c1, wqkv, bq, bv, a1, qkv, weights, mixed, narrow, gb2, padded):
        fill_masked(padded, cot, count[0], stride)
        gb2[...] = jnp.sum(padded[...], axis=0, keepdims=True)
        narrow[...] = padded[...].astype(BF16)
        fill_padded(padded, x, stride)

        @pl.loop(0, total // CHUNK)
        def _(i):
            normed, _ = row_norm(padded[rows_of(i), :])
            a1[rows_of(i), :] = (normed * g1[...] + c1[...]).astype(BF16)

        qkv[:, :D] = (dot(a1[...], wqkv[:, :D]) + bq[...]).astype(BF16)
        qkv[:, D : 2 * D] = dot(a1[...], wqkv[:, D : 2 * D]).astype(BF16)
        qkv[:, 2 * D :] = (dot(a1[...], wqkv[:, 2 * D :]) + bv[...]).astype(BF16)
        hidden = lax.broadcasted_iota(jnp.int32, (stride, stride), 1) >= tokens

        @pl.loop(0, slots * pairs)
        def _(i):
            query = qkv[head_rows(i), head_columns(i, 0)]
            key = qkv[head_rows(i), head_columns(i, 1)]
            value = qkv[head_rows(i), head_columns(i, 2)]
            outs = []
            for part in range(2):
                masked = jnp.where(lane_mask(part), query, jnp.zeros_like(query))
                scores = dot(masked, key, NT) * qk_scale
                scores = jnp.where(hidden, -1e30, scores)
                top = jnp.max(scores, axis=-1, keepdims=True)
                log_total = top + jnp.log(
                    jnp.sum(jnp.exp(scores - top), axis=-1, keepdims=True)
                )
                soft = jnp.exp(scores - log_total)
                weights[2 * i + part] = soft
                outs.append(dot(soft.astype(BF16), value))
            mixed[head_rows(i), head_columns(i, 0)] = jnp.where(
                lane_mask(0), outs[0], outs[1]
            ).astype(BF16)

    a1, qkv, weights, mixed, narrow, gb2 = call(
        attend,
        [
            array((total, D), BF16),
            array((total, 3 * D), BF16),
            array((slots * heads, stride, stride)),
            array((total, D), BF16),
            array((total, D), BF16),
            array((1, D)),
        ],
        [counts, inputs, cotangent, w["g1"], w["c1"], w["wqkv"], w["bq"], w["bv"]],
        [pltpu.VMEM((total, D), F32)],
        scalars=1,
        flops=8 * total * D * D,
    )

    width = 512

    def widen(x, mixed, wo, bo, g2, c2, w1, b1, middle, a2, rows, slope, block):
        fill_padded(middle, x, stride)
        middle[...] = middle[...] + (dot(mixed[...], wo[...]) + bo[...])

        @pl.loop(0, total // CHUNK)
        def _(i):
            normed, _ = row_norm(middle[rows_of(i), :])
            a2[rows_of(i), :] = (normed * g2[...] + c2[...]).astype(BF16)

        @pl.loop(0, FF // width)
        def _(j):
            columns = rows_of(j, width)
            block[...] = dot(a2[...], w1[:, columns]) + b1[:, columns]

            @pl.loop(0, total // CHUNK)
            def _(i):
                value = block[rows_of(i), :]
                phi = 0.5 * (1.0 + lax.erf(value * INV_ROOT_TWO))
                rows[rows_of(i), columns] = (value * phi).astype(BF16)
                slope[rows_of(i), columns] = (
                    phi + value * jnp.exp(-0.5 * value * value) * INV_ROOT_TWOPI
                )

    middle, a2, rows, slope = call(
        widen,
        [
            array((total, D)),
            array((total, D), BF16),
            array((total, FF), BF16),
            array((total, FF)),
        ],
        [inputs, mixed, w["wo"], w["bo"], w["g2"], w["c2"], w["w1"], w["b1"]],
        [pltpu.VMEM((total, width), F32)],
        flops=10 * total * D * D,
    )
    factors = {"w2": (rows, narrow)}
    vectors = {"b2": gb2}
    narrow = pack(3, factors, vectors, narrow)

    def finish(middle, rows, slope, narrow, w2, b2, out, d_pre, gb1):
        final = middle[...] + (dot(rows[...], w2[...]) + b2[...])
        for s in range(slots):
            out[s] = final[s * stride : s * stride + tokens, :]

        @pl.loop(0, FF // width)
        def _(j):
            columns = rows_of(j, width)
            grad = dot(narrow[...], w2[columns, :], NT) * slope[:, columns]
            d_pre[:, columns] = grad.astype(BF16)
            gb1[:, columns] = jnp.sum(grad, axis=0, keepdims=True)

    outputs, d_pre, gb1 = call(
        finish,
        [array(inputs.shape), array((total, FF), BF16), array((1, FF))],
        [middle, rows, slope, narrow, w["w2"], w["b2"]],
        flops=16 * total * D * D,
    )
    factors["w1"] = (a2, d_pre)
    vectors["b1"] = gb1
    d_pre = pack(2, factors, vectors, d_pre)

    def back_middle(
        count, cot, middle, d_pre, w1, wo, g2, d_mid, d_narrow, d_mixed, gg2, gc2, gbo, work
    ):
        work[...] = dot(d_pre[...], w1[...], NT)
        gc2[...] = jnp.sum(work[...], axis=0, keepdims=True)
        gg2[...] = jnp.zeros_like(gg2)
        fill_masked(d_mid, cot, count[0], stride)

        @pl.loop(0, total // CHUNK)
        def _(i):
            back, gain = row_norm_back(work[rows_of(i), :], middle[rows_of(i), :], g2[...])
            gg2[...] += gain
            grad = d_mid[rows_of(i), :] + back
            d_mid[rows_of(i), :] = grad
            d_narrow[rows_of(i), :] = grad.astype(BF16)

        gbo[...] = jnp.sum(d_mid[...], axis=0, keepdims=True)
        d_mixed[...] = dot(d_narrow[...], wo[...], NT).astype(BF16)

    d_mid, d_narrow, d_mixed, gg2, gc2, gbo = call(
        back_middle,
        [
            array((total, D)),
            array((total, D), BF16),
            array((total, D), BF16),
            array((1, D)),
            array((1, D)),
            array((1, D)),
        ],
        [counts, cotangent, middle, d_pre, w["w1"], w["wo"], w["g2"]],
        [pltpu.VMEM((total, D), F32)],
        scalars=1,
        flops=10 * total * D * D,
    )
    factors["wo"] = (mixed, d_narrow)
    vectors.update(bo=gbo, g2=gg2, c2=gc2)
    d_mixed = pack(1, factors, vectors, d_mixed)

    def back_attend(
        x, qkv, weights, d_mixed, d_mid, wqkv, g1, d_proj, grad_in, gbq, gbv, gg1, gc1, padded, work
    ):
        gbq[...] = jnp.zeros_like(gbq)
        gbv[...] = jnp.zeros_like(gbv)

        @pl.loop(0, slots * pairs)
        def _(i):
            query = qkv[head_rows(i), head_columns(i, 0)]
            key = qkv[head_rows(i), head_columns(i, 1)]
            value = qkv[head_rows(i), head_columns(i, 2)]
            grad = d_mixed[head_rows(i), head_columns(i, 0)]
            found = []
            for part in range(2):
                soft = weights[2 * i + part]
                masked = jnp.where(lane_mask(part), grad, jnp.zeros_like(grad))
                d_soft = dot(masked, value, NT)
                row_dot = jnp.sum(soft * d_soft, axis=-1, keepdims=True)
                d_scores = (soft * (d_soft - row_dot) * qk_scale).astype(BF16)
                found.append(
                    (
                        dot(d_scores, key),
                        dot(d_scores, query, TN),
                        dot(soft.astype(BF16), grad, TN),
                    )
                )
            joined = [jnp.where(lane_mask(0), a, b) for a, b in zip(*found)]
            for part in range(3):
                d_proj[head_rows(i), head_columns(i, part)] = joined[part].astype(BF16)
            gbq[:, head_columns(i, 0)] += jnp.sum(joined[0], axis=0, keepdims=True)
            gbv[:, head_columns(i, 0)] += jnp.sum(joined[2], axis=0, keepdims=True)

        work[...] = dot(d_proj[...], wqkv[...], NT)
        gc1[...] = jnp.sum(work[...], axis=0, keepdims=True)
        gg1[...] = jnp.zeros_like(gg1)
        fill_padded(padded, x, stride)

        @pl.loop(0, total // CHUNK)
        def _(i):
            back, gain = row_norm_back(work[rows_of(i), :], padded[rows_of(i), :], g1[...])
            gg1[...] += gain
            work[rows_of(i), :] = d_mid[rows_of(i), :] + back

        for s in range(slots):
            grad_in[s] = work[s * stride : s * stride + tokens, :]

    d_proj, input_grad, gbq, gbv, gg1, gc1 = call(
        back_attend,
        [
            array((total, 3 * D), BF16),
            array(inputs.shape),
            array((1, D)),
            array((1, D)),
            array((1, D)),
            array((1, D)),
        ],
        [inputs, qkv, weights, d_mixed, d_mid, w["wqkv"], w["g1"]],
        [pltpu.VMEM((total, D), F32)] * 2,
        flops=8 * total * D * D,
    )
    factors["wqkv"] = (a1, d_proj)
    vectors.update(bq=gbq, bv=gbv, g1=gg1, c1=gc1)
    pack(0, factors, vectors, d_proj)
    return outputs, input_grad


def adam_update(params, grads, moment_one, moment_two):
    new_one = BETA_ONE * moment_one + (1.0 - BETA_ONE) * grads
    new_two = BETA_TWO * moment_two + (1.0 - BETA_TWO) * grads * grads
    fix_one = 1.0 - BETA_ONE**ADAM_STEP
    fix_two = 1.0 - BETA_TWO**ADAM_STEP
    update = new_one / fix_one / (jnp.sqrt(new_two / fix_two) + EPS_ADAM)
    return (params - RATE * (update + DECAY * params), new_one, new_two)


def local(plan, *operands):
    return layer_step(plan, *operands)


def layer_step(plan, inputs, cotangent, counts, params, moment_one, moment_two):
    me = lax.axis_index("fsdp")
    rows = params.reshape(plan.rows, LANES)
    narrow = jnp.pad(rows.astype(BF16), ((0, plan.padded - plan.rows), (0, 0)))
    gathered = gather_quarters(narrow, plan, me)
    position = (me % plan.low).astype(jnp.int32).reshape(1)
    weights = {}
    for names in GROUPS:
        weights.update(unpack_group(names, gathered, plan, position))
    summed = {}

    def pack(q, factors, vectors, after):
        packed = pack_quarter(q, factors, vectors, plan)
        packed, after = tie(packed, after)
        summed[q] = scatter_quarter(packed, plan, me)
        return after

    outputs, input_grad = run_block(counts, inputs, cotangent, weights, pack)
    shard_grad = scatter_across(summed, plan, me)
    new_params, new_one, new_two = adam_update(
        rows,
        shard_grad,
        moment_one.reshape(plan.rows, LANES),
        moment_two.reshape(plan.rows, LANES),
    )
    flat = lambda array: array.reshape(-1)
    return (outputs, input_grad, flat(shard_grad), flat(new_params), flat(new_one), flat(new_two))


def solution(mesh):
    devices = mesh.shape["fsdp"]

    def step(inputs, cotangent, counts, params, moment_one, moment_two):
        plan = Plan(devices, params.shape[0] // devices)
        placed = (P("fsdp", None, None),) * 2 + (P("fsdp"),) * 4
        return jax.shard_map(
            functools.partial(local, plan),
            mesh=mesh,
            in_specs=placed,
            out_specs=placed,
            check_vma=False,
        )(inputs, cotangent, counts, params, moment_one, moment_two)

    return step
```
